512 devices in a mesh: row: 32 (over y, z_hi, x), col: 16 (over z_lo, core).
Axes of the slice: x: 4, y: 4, z: 16 (z_hi: 2, z_lo: 8; z = z_hi * 8 + z_lo), core: 2. Of those that a mesh axis runs over, the one named last changes fastest.
Arguments:
- nodes: bfloat16 [2048, 512], P(('row', 'col')), may hold values from -50 to 50
- coords: float32 [3, 2048], P(None, ('row', 'col')), may hold values from -18 to 18
- atom_types: int32 [2048], P(('row', 'col')), may hold values from 0 to 29
- segment_ids: int32 [2048], P(('row', 'col')), may hold values from 0 to 1
- pair_mask: int32 [2048, 2048], P('row', 'col'), may hold values 0 or 1
- pair_bias: bfloat16 [64, 2048, 2048], P(None, 'row', 'col'), may hold values from -10 to 310
- ln_gain: float32 [512], replicated, may hold values from 0.1 to 1.9
- w_qkv: bfloat16 [512, 1536], replicated, may hold values from -0.25 to 0.25
- gauss_mul: float32 [60, 60], replicated, may hold values from 0.25 to 1.75
- gauss_add: float32 [60, 60], replicated, may hold values from -4 to 4
- gauss_mean: float32 [128], replicated, may hold values from 0 to 16
- gauss_width: float32 [128], replicated, may hold values from 0.5 to 2.5
- w_gauss: bfloat16 [128, 128], replicated, may hold values from -2 to 2
- w_heads: bfloat16 [128, 64], replicated, may hold values from -2 to 2
- w_coord1: bfloat16 [64, 64], replicated, may hold values from -0.75 to 0.75
- w_coord2: bfloat16 [64], replicated, may hold values from -0.75 to 0.75
Outputs:
- attended: bfloat16 [2048, 512], P(('row', 'col'))
- moved: float32 [3, 2048], P(None, ('row', 'col'))
The draws below stay inside these ranges and needn't reach their ends.
All inputs are finite; a program needn't handle non-finite values. No bound on the sum of `pair_mask` on one device may be relied on, other than what follows from the above.
Results may differ from the reference program's by a relative error of at most 0.015.
Values may be sent and summed in bfloat16 or wider, within the bound.
A program may use at most 64 MiB of HBM per device.

```python
import math
import jax
import jax.numpy as jnp
from jax import lax

D = 512
HEADS = 64
GAUSS = 128
ATOM_TYPES = 30
KINDS = 60
ATOMS = 2048
N_ROW = 32


def draw_nodes(key, part):
    base_key = jax.random.fold_in(key, 11)
    column_key = jax.random.fold_in(key, 12)
    row_key = jax.random.fold_in(key, 13)
    column_scale = jnp.exp(jax.random.uniform(column_key, (1, D), jnp.float32, -1.15, 1.15))
    row_scale = jnp.exp(jax.random.uniform(row_key, (ATOMS, 1), jnp.float32, -1.15, 1.15))
    values = jnp.clip(jax.random.normal(base_key, (ATOMS, D), jnp.float32), -5.0, 5.0)
    return (values * column_scale * row_scale).astype(jnp.bfloat16)


def draw_pair_bias(key, part):
    base_key = jax.random.fold_in(key, 21)
    full_shape = (HEADS, ATOMS, ATOMS)
    values = jnp.clip(jax.random.normal(base_key, full_shape, jnp.float32) * 2.0, -10.0, 10.0)
    return values.astype(jnp.bfloat16)


def plant(result, key, least, top_value):
    index_at = [jax.random.randint(jax.random.fold_in(key, axis), (), 0, length) for axis, length in enumerate(result.shape)]
    widest = result.shape.index(max(result.shape))
    neighbour = index_at[:widest] + [(index_at[widest] + 1) % result.shape[widest]] + index_at[widest + 1:]
    return result.at[tuple(index_at)].set(least).at[tuple(neighbour)].set(top_value)


def block_levels(rng, shape, pieces, least, largest):
    gain, own = 1.0, jax.random.fold_in(rng, 6)
    for axis_at, shards_of in pieces:
        draws = jnp.exp(jax.random.uniform(jax.random.fold_in(own, axis_at), (shards_of,), jnp.float32, least / len(pieces), largest / len(pieces)))
        gain = gain * jnp.repeat(draws, shape[axis_at] // shards_of).reshape([-1 if axis == axis_at else 1 for axis in range(len(shape))])
    return gain


def noise(own_key, dims, width, reach, split=(), kind=jnp.bfloat16):
    drawn = jax.random.normal(own_key, dims, jnp.float32) * width
    if len(split) > 0:
        drawn = block_levels(own_key, dims, split, -0.22, 0.18) * drawn
    return jnp.clip(drawn, min=-reach, max=reach).astype(kind)


def setup_inputs(seed: int = 0) -> dict:
    keys = jax.random.split(jax.random.key(seed), 17)
    return {
        "nodes": draw_nodes(jax.random.fold_in(keys[16], 71), 0),
        "coords": noise(keys[1], (3, ATOMS), 3.0, 18.0, ((1, 512),), jnp.float32),
        "atom_types": plant(jax.random.randint(keys[2], (ATOMS,), 0, ATOM_TYPES), jax.random.fold_in(keys[2], 1), 0, ATOM_TYPES - 1).astype(jnp.int32),
        "segment_ids": plant(jax.random.randint(keys[3], (ATOMS,), 0, 2), jax.random.fold_in(keys[3], 1), 0, 1).astype(jnp.int32),
        "pair_mask": plant((jax.random.randint(keys[4], (ATOMS, ATOMS), 0, 8) < 7).astype(jnp.int32), jax.random.fold_in(keys[4], 1), 0, 1),
        "pair_bias": draw_pair_bias(jax.random.fold_in(keys[16], 71), 0),
        "ln_gain": jnp.clip(1.0 + 0.18 * jax.random.normal(keys[6], (D,), jnp.float32), 0.1, 1.9),
        "w_qkv": noise(keys[7], (D, 3 * D), D ** -0.5, 0.25),
        "gauss_mul": jnp.clip(1.0 + 0.15 * jax.random.normal(keys[8], (KINDS, KINDS), jnp.float32), 0.25, 1.75),
        "gauss_add": noise(keys[9], (KINDS, KINDS), 1.0, 4.0, (), jnp.float32),
        "gauss_mean": jnp.clip(jax.random.uniform(keys[10], (GAUSS,), jnp.float32, 0.0, 16.0), 0.0, 16.0),
        "gauss_width": jnp.clip(jnp.exp(jax.random.uniform(keys[11], (GAUSS,), jnp.float32, math.log(0.5), math.log(2.5))), 0.5, 2.5),
        "w_gauss": noise(keys[12], (GAUSS, GAUSS), (GAUSS // 16) ** -0.5, 2.0),
        "w_heads": noise(keys[13], (GAUSS, HEADS), (GAUSS // 16) ** -0.5, 2.0),
        "w_coord1": noise(keys[14], (HEADS, HEADS), HEADS ** -0.5, 0.75),
        "w_coord2": noise(keys[15], (HEADS,), HEADS ** -0.5, 0.75),
    }


ln_epsilon = 1e-05
masked_fill = -1000000000.0
root_shift = 0.01

def widened(values):
    return lax.optimization_barrier(values).astype(jnp.float32)

def layer_normed(nodes, ln_gain):
    features = nodes.astype(jnp.float32)
    row_mean = lax.optimization_barrier(jnp.mean(features, axis=1, keepdims=True))
    centred = features - row_mean
    spread = lax.optimization_barrier(jnp.mean(centred * centred, axis=1, keepdims=True))
    return (centred * lax.rsqrt(spread + ln_epsilon) * ln_gain[None, :]).astype(jnp.bfloat16)

def gaussians(expanded, gauss_mean, gauss_width):
    scaled = (expanded[None, :, :] - gauss_mean[:, None, None]) / gauss_width[:, None, None]
    norming = math.sqrt(2.0 * math.pi) * gauss_width[:, None, None]
    return (jnp.exp(-0.5 * scaled * scaled) / norming).astype(jnp.bfloat16)

def reference(nodes, coords, atom_types, segment_ids, pair_mask, pair_bias, ln_gain, w_qkv, gauss_mul, gauss_add, gauss_mean, gauss_width, w_gauss, w_heads, w_coord1, w_coord2):
    head_dim = D // HEADS
    normed = layer_normed(nodes, ln_gain)
    projected = jnp.dot(normed, w_qkv, preferred_element_type=jnp.float32).astype(jnp.bfloat16)
    queries = widened(projected[:, :D]).reshape(ATOMS, HEADS, head_dim)
    keys_all = widened(projected[:, D:2 * D]).reshape(ATOMS, HEADS, head_dim)
    values_all = widened(projected[:, 2 * D:]).reshape(ATOMS, HEADS, head_dim)
    kinds = atom_types + ATOM_TYPES * segment_ids
    block_rows = ATOMS // N_ROW

    def one_block(block_index):
        start_row = (block_index * block_rows).astype(jnp.int32)
        query_block = lax.dynamic_slice_in_dim(queries, start_row, block_rows, 0)
        coord_block = lax.dynamic_slice_in_dim(coords, start_row, block_rows, 1)
        kind_block = lax.dynamic_slice_in_dim(kinds, start_row, block_rows, 0)
        bias_block = lax.dynamic_slice_in_dim(pair_bias, start_row, block_rows, 1)
        mask_block = lax.dynamic_slice_in_dim(pair_mask, start_row, block_rows, 0)
        offsets = coord_block[:, :, None] - coords[:, None, :]
        distance = jnp.sqrt(lax.optimization_barrier(jnp.sum(offsets * offsets, axis=0)) + root_shift)
        expanded = gauss_mul[kind_block[:, None], kinds[None, :]] * distance + gauss_add[kind_block[:, None], kinds[None, :]]
        features = gaussians(expanded, gauss_mean, gauss_width)
        hidden = jax.nn.gelu(jnp.einsum('kij,kl->lij', widened(features), w_gauss.astype(jnp.float32))).astype(jnp.bfloat16)
        geometry = jnp.einsum('kij,kh->hij', widened(hidden), w_heads.astype(jnp.float32))
        affinity = jnp.einsum('ihd,jhd->hij', query_block, keys_all) / math.sqrt(head_dim)
        logits = bias_block.astype(jnp.float32) + geometry + affinity
        pair_new = logits.astype(jnp.bfloat16)
        masked = jnp.where(mask_block[None, :, :] == 1, logits, masked_fill)
        weights = jnp.exp(masked - lax.optimization_barrier(jnp.max(masked, axis=2, keepdims=True)))
        denominator = lax.optimization_barrier(jnp.sum(weights, axis=2))
        numerator = jnp.einsum('hij,jhd->ihd', widened(weights.astype(jnp.bfloat16)), values_all)
        attended = (numerator / denominator.T[:, :, None]).reshape(block_rows, D).astype(jnp.bfloat16)
        mixed = jax.nn.gelu(jnp.einsum('hij,hg->gij', widened(pair_new), w_coord1.astype(jnp.float32))).astype(jnp.bfloat16)
        strength = jnp.einsum('gij,g->ij', widened(mixed), w_coord2.astype(jnp.float32))
        strength = jnp.where(mask_block == 1, strength, 0.0)
        row_total = lax.optimization_barrier(jnp.sum(strength, axis=1))
        pulled = jnp.dot(strength, coords.T, precision=lax.Precision.HIGHEST)
        displace = (coord_block.T * row_total[:, None] - pulled) / ATOMS
        return (attended, displace)
    attended, displace = lax.map(one_block, jnp.arange(N_ROW, dtype=jnp.int32))
    attended = attended.reshape(ATOMS, D)
    moved = coords + displace.reshape(ATOMS, 3).T
    return (attended, moved)
```

```python
import functools
import math

import jax
import jax.numpy as jnp
from jax import lax
from jax.experimental import pallas as pl
from jax.experimental.pallas import tpu as pltpu
from jax.sharding import PartitionSpec as P

MESH = pl.DeviceIdType.MESH
F32 = jnp.float32
BF16 = jnp.bfloat16
ln_epsilon = 1e-05
masked_fill = -1000000000.0
root_shift = 0.01
GELU_A = math.sqrt(2.0 / math.pi)
GELU_B = GELU_A * 0.044715


def gelu(x):
    half = 0.5 * x
    return half + half * jnp.tanh(x * (GELU_A + GELU_B * (x * x)))


def nt_dot(a, b):
    return lax.dot_general(a, b, (((1,), (1,)), ((), ())), preferred_element_type=F32)


def nn_dot(a, b, precision=None):
    return jnp.dot(a, b, preferred_element_type=F32, precision=precision)


def lanes(shape):
    return lax.broadcasted_iota(jnp.int32, shape, len(shape) - 1)


def layer_norm(nodes, gain):
    x = nodes.astype(F32)
    centred = x - jnp.mean(x, axis=1, keepdims=True)
    spread = jnp.mean(centred * centred, axis=1, keepdims=True)
    return (centred * lax.rsqrt(spread + ln_epsilon) * gain).astype(BF16)


def prepare(w):
    w.wg_t[...] = w.w_gauss[...].astype(F32).T.astype(BF16)
    w.w1_t[...] = w.w_coord1[...].astype(F32).T.astype(BF16)
    w2 = w.w_coord2[...].astype(F32)
    wide = jnp.concatenate([w2] * 8, axis=1)
    own = lanes((8, 512)) // 64 == lax.broadcasted_iota(jnp.int32, (8, 512), 0)
    w.w2_b[...] = jnp.where(own, jnp.broadcast_to(wide, (8, 512)), 0.0).astype(BF16)
    mean = jnp.broadcast_to(w.gauss_mean[...], (128, 128)).T
    width = jnp.broadcast_to(w.gauss_width[...], (128, 128)).T
    slope = math.sqrt(0.5 * math.log2(math.e)) / width
    w.g_a[...] = slope
    w.g_b[...] = slope * mean
    w.g_c[...] = -jnp.log2(math.sqrt(2.0 * math.pi) * width)


def joined(parts):
    return parts + pltpu.roll(parts, 120, 1) + pltpu.roll(parts, 112, 1)


def pair_distances(w):
    for s in range(w.q_nodes.shape[0]):
        w.q_f[4 * s : 4 * s + 4, :] = w.q_nodes[s].astype(F32)
    for s in range(w.k_nodes.shape[0]):
        w.k_f[4 * s : 4 * s + 4, :] = w.k_nodes[s].astype(F32)
    qt = joined(w.q_f[:, 512:640])
    w.q_t[...] = qt
    kt = joined(w.k_f[:, 512:640]).T
    w.k_row[...] = kt[0:8, :]
    total = root_shift
    for axis in range(3):
        offset = qt[:, axis : axis + 1] - kt[axis : axis + 1, :]
        total = total + offset * offset
    distance = jnp.sqrt(total)
    kinds = w.gauss_mul.shape[0]
    q_hot = (lanes((64, kinds)).astype(F32) == qt[:, 3:4]).astype(F32)
    k_hot = (lax.broadcasted_iota(jnp.int32, (kinds, 128), 0).astype(F32) == kt[3:4, :]).astype(F32)
    high = lax.Precision.HIGHEST
    scale = nn_dot(nn_dot(q_hot, w.gauss_mul[...], high), k_hot, high)
    shift = nn_dot(nn_dot(q_hot, w.gauss_add[...], high), k_hot, high)
    w.expanded[...] = scale * distance + shift


def geometry(w):
    step = 8

    def chunk(c, carry):
        base = pl.multiple_of(c * step, step)
        rows = w.expanded[pl.ds(base, step), :]
        a, b, k = w.g_a[...], w.g_b[...], w.g_c[...]
        parts = []
        for i in range(step):
            t = a * rows[i : i + 1, :] - b
            parts.append(jnp.exp2(k - t * t).astype(BF16))
        features = jnp.concatenate(parts, axis=1)
        hidden = gelu(nn_dot(w.wg_t[...], features)).astype(BF16)
        geo = nn_dot(w.w_heads[...], hidden)
        for i in range(step):
            w.logits[pl.ds(base + i, 64, stride=64), :] = geo[:, 128 * i : 128 * i + 128]
        return carry

    lax.fori_loop(0, 64 // step, chunk, 0)


def project(w):
    qn = w.q_f[:, 0:512].astype(BF16)
    kn = w.k_f[:, 0:512].astype(BF16)
    w.q_p[...] = nn_dot(qn, w.w_qkv[:, 0:512]).astype(BF16)
    w.k_p[...] = nn_dot(kn, w.w_qkv[:, 512:1024]).astype(BF16)
    w.v_p[...] = nn_dot(kn, w.w_qkv[:, 1024:1536]).astype(BF16)


def attention(w):
    take = w.mask[...] == 1
    lane = lanes((64, 128))
    ones = jnp.ones((128, 128), BF16)
    scale = 1.0 / math.sqrt(8.0)
    per = 4
    maxima = jnp.zeros((64, 128), F32)
    totals = jnp.ones((64, 128), F32)
    for g in range(4):
        cols = slice(128 * g, 128 * g + 128)
        q_g = w.q_p[:, cols].astype(F32)
        k_g = w.k_p[:, cols]
        v_g = jnp.concatenate([w.v_p[:, cols], ones], axis=1)

        def heads(n, carry, g=g, q_g=q_g, k_g=k_g, v_g=v_g):
            maxima, totals, num, den = carry
            sel = [(lane >> 3) == n * per + u for u in range(per)]
            left = jnp.concatenate([jnp.where(s, q_g, 0.0).astype(BF16) for s in sel], axis=0)
            affinity = nt_dot(left, k_g)
            probs = []
            tops = []
            for u in range(per):
                head = g * 16 + n * per + u
                at = pl.ds(pl.multiple_of(head * 64, 64), 64)
                logit = (
                    w.bias[head].astype(F32)
                    + w.logits[at, :]
                    + affinity[64 * u : 64 * u + 64] * scale
                )
                w.logits[at, :] = logit
                masked = jnp.where(take, logit, masked_fill)
                top = jnp.max(masked, axis=1, keepdims=True)
                tops.append(top)
                probs.append(jnp.exp(masked - top).astype(BF16))
            out = nn_dot(jnp.concatenate(probs, axis=0), v_g)
            for u in range(per):
                head = g * 16 + n * per + u
                part = out[64 * u : 64 * u + 64]
                num = jnp.where(sel[u], part[:, 0:128], num)
                den = jnp.where(sel[u], part[:, 128:256], den)
                here = lane == head
                maxima = jnp.where(here, tops[u], maxima)
                totals = jnp.where(here, part[:, 128:256], totals)
            return maxima, totals, num, den

        zero = jnp.zeros((64, 128), F32)
        maxima, totals, num, den = lax.fori_loop(0, 16 // per, heads, (maxima, totals, zero, zero))
        part = num / den
        for s in range(16):
            w.att_s[s, :, cols] = part[4 * s : 4 * s + 4].astype(BF16)
    stat = maxima + jnp.log(totals)
    for s in range(16):
        w.lse_s[s] = stat[4 * s : 4 * s + 4]


def displacement(w):
    step = 8

    def chunk(c, carry):
        base = pl.multiple_of(c * step, step)
        parts = [w.logits[pl.ds(base + i, 64, stride=64), :].astype(BF16) for i in range(step)]
        mixed = gelu(nn_dot(w.w1_t[...], jnp.concatenate(parts, axis=1))).astype(BF16)
        stacked = jnp.concatenate([mixed[:, 128 * i : 128 * i + 128] for i in range(step)], axis=0)
        w.strength[pl.ds(base, step), :] = nn_dot(w.w2_b[...], stacked)
        return carry

    lax.fori_loop(0, 64 // step, chunk, 0)
    strength = jnp.where(w.mask[...] == 1, w.strength[...], 0.0)
    qt = w.q_t[...]
    lane = lanes((64, 128))
    out = jnp.zeros((64, 128), F32)
    for axis in range(3):
        offset = qt[:, axis : axis + 1] - w.k_row[axis : axis + 1, :]
        moved = jnp.sum(strength * offset, axis=1, keepdims=True) * (1.0 / w.atoms)
        out = jnp.where(lane == axis, moved, out)
    for s in range(16):
        w.dis_s[s] = out[4 * s : 4 * s + 4]


def combine_attended(w):
    count = 16
    top = w.lse_r[0]
    for s in range(1, count):
        top = jnp.maximum(top, w.lse_r[s])
    total = jnp.zeros((4, 128), F32)
    for s in range(count):
        e = jnp.exp(w.lse_r[s] - top)
        w.coef[4 * s : 4 * s + 4, :] = e
        total = total + e
    inverse = 1.0 / total
    for s in range(count):
        w.coef[4 * s : 4 * s + 4, :] = w.coef[4 * s : 4 * s + 4, :] * inverse
    spread = (lanes((128, 512)) // 8 == lax.broadcasted_iota(jnp.int32, (128, 512), 0)).astype(BF16)
    coef = w.coef[...]
    top_part = coef.astype(BF16)
    rest = (coef - top_part.astype(F32)).astype(BF16)
    w.q_f[:, 0:512] = nn_dot(top_part, spread) + nn_dot(rest, spread)
    result = jnp.zeros((4, 512), F32)
    for s in range(count):
        result = result + w.q_f[4 * s : 4 * s + 4, 0:512] * w.att_r[s].astype(F32)
    return result.astype(BF16)


def combine_moved(w):
    total = w.dis_r[0]
    for s in range(1, 16):
        total = total + w.dis_r[s]
    w.pad[0:4, :] = total
    w.pad_t[...] = w.pad[...].T
    return w.coords[...] + w.pad_t[0:3, 0:4]


LOADED = dict(
    nodes=((4, 512), BF16),
    coords=((3, 4), F32),
    types=((1, 4), jnp.int32),
    segments=((1, 4), jnp.int32),
    ln_gain=((1, 512), F32),
    gauss_mean=((1, 128), F32),
    gauss_width=((1, 128), F32),
    w_gauss=((128, 128), BF16),
    w_coord1=((64, 64), BF16),
    w_coord2=((1, 64), BF16),
    gauss_mul=((60, 60), F32),
    gauss_add=((60, 60), F32),
    w_heads=((64, 128), BF16),
    mask=((64, 128), jnp.int32),
    w_qkv=((512, 1536), BF16),
    bias=((64, 64, 128), BF16),
)
WORK = dict(
    wg_t=((128, 128), BF16),
    w1_t=((64, 64), BF16),
    w2_b=((8, 512), BF16),
    g_a=((128, 128), F32),
    g_b=((128, 128), F32),
    g_c=((128, 128), F32),
    q_t=((64, 128), F32),
    k_row=((8, 128), F32),
    expanded=((64, 128), F32),
    logits=((4096, 128), F32),
    q_f=((64, 640), F32),
    k_f=((128, 640), F32),
    q_p=((64, 512), BF16),
    k_p=((128, 512), BF16),
    v_p=((128, 512), BF16),
    strength=((64, 128), F32),
    coef=((64, 128), F32),
    pad=((128, 128), F32),
    pad_t=((128, 128), F32),
    own=((4, 640), BF16),
    q_nodes=((16, 4, 640), BF16),
    k_nodes=((32, 4, 640), BF16),
    att_s=((16, 4, 512), BF16),
    lse_s=((16, 4, 128), F32),
    dis_s=((16, 4, 128), F32),
    att_r=((16, 4, 512), BF16),
    lse_r=((16, 4, 128), F32),
    dis_r=((16, 4, 128), F32),
)


class Refs:
    pass


def own_block(w):
    w.own[:, 0:512] = layer_norm(w.nodes[...], w.ln_gain[...])
    w.pad[...] = jnp.zeros((128, 128), F32)
    rest = w.coords[...]
    for part in range(3):
        piece = rest.astype(BF16).astype(F32)
        w.pad[8 * part : 8 * part + 3, 0:4] = piece
        rest = rest - piece
    kinds = w.types[...] + w.gauss_mul.shape[0] // 2 * w.segments[...]
    w.pad[3:4, 0:4] = kinds.astype(F32)
    w.pad_t[...] = w.pad[...].T
    w.own[:, 512:640] = w.pad_t[0:4, :].astype(BF16)


def kernel(rows, cols, *refs):
    w = Refs()
    count = len(LOADED)
    sources, refs = refs[:count], refs[count:]
    w.attended, w.moved = refs[:2]
    refs = refs[2:]
    for name, ref in zip([*LOADED, *WORK], refs):
        setattr(w, name, ref)
    load_sem, kz_send, kz_recv, kx_send, kx_recv, qn_send, qn_recv = refs[-13:-6]
    at_send, at_recv, ls_send, ls_recv, ds_send, ds_recv = refs[-6:]
    w.atoms = float(rows * cols * 4)
    row, col = lax.axis_index("row"), lax.axis_index("col")
    x, line = lax.rem(row, 4), lax.rem(row // 4, 2)
    level, core = col // 2, lax.rem(col, 2)
    home = row // 2
    own_key = home == col
    relay = core == x // 2
    half = lax.rem(x, 2)
    planes = rows // 4
    source_row = level * 4 + x

    def with_x(other):
        return row - x + other

    barrier = pltpu.get_barrier_semaphore()

    def greet(r, c):
        pl.semaphore_signal(barrier, inc=1, device_id=(r, c), device_id_type=MESH)

    def greet_row(n, carry):
        greet(row, lax.rem(col + n, cols))
        return carry

    @pl.when(relay)
    def _():
        def greet_source(n, carry):
            @pl.when(jnp.logical_not(jnp.logical_and(source_row == row, n == col)))
            def _():
                greet(source_row, n)

            return carry

        lax.fori_loop(0, cols, greet_source, 0)

    lax.fori_loop(1, cols, greet_row, 0)
    for side in range(2):
        other = 2 * core + side

        @pl.when(other != x)
        def _(other=other):
            greet(with_x(other), col)

    loads = []
    for n, (name, source) in enumerate(zip(LOADED, sources, strict=True)):
        loads.append(pltpu.make_async_copy(source, getattr(w, name), load_sem.at[n]))
        loads[-1].start()
    for load in loads[:-2]:
        load.wait()
    own_block(w)
    prepare(w)

    pl.semaphore_wait(
        barrier, cols - 1 + planes - jnp.where(own_key, 1, 0) + jnp.where(relay, 3, 0)
    )

    def far_copy(n):
        plane = lax.rem(row // 4 + n, planes)
        return pltpu.make_async_remote_copy(
            src_ref=w.own,
            dst_ref=w.k_nodes.at[half * cols + col],
            send_sem=kz_send.at[n],
            recv_sem=kz_recv.at[col],
            device_id=(plane * 4 + x, home),
            device_id_type=MESH,
        )

    def far_copies(act):
        def one(n, carry):
            act(far_copy(n))
            return carry

        lax.fori_loop(1, planes, one, 0)

        @pl.when(jnp.logical_not(own_key))
        def _():
            act(far_copy(0))

    def relay_copy(pair, step):
        part = w.k_nodes.at[pl.ds(half * cols + 2 * pair, 2)]
        return pltpu.make_async_remote_copy(
            src_ref=part,
            dst_ref=part,
            send_sem=kx_send.at[pair * 3 + step - 1],
            recv_sem=kx_recv.at[half * (cols // 2) + pair],
            device_id=(with_x(lax.rem(x + step, 4)), col),
            device_id_type=MESH,
        )

    def row_copy(src, dst, send, recv, n):
        c = lax.rem(col + n, cols)
        return pltpu.make_async_remote_copy(
            src_ref=src(c),
            dst_ref=dst.at[col],
            send_sem=send.at[n],
            recv_sem=recv.at[col],
            device_id=(row, c),
            device_id_type=MESH,
        )

    def row_copies(src, dst, send, recv, act):
        def one(n, carry):
            act(row_copy(src, dst, send, recv, n))
            return carry

        lax.fori_loop(1, cols, one, 0)

    def start(copy):
        copy.start()

    def sent(copy):
        copy.wait_send()

    def wait_row(src, dst, recv):
        def one(n, carry):
            c = lax.rem(col + n, cols)
            pltpu.make_async_copy(src(c), dst.at[c], recv.at[c]).wait()
            return carry

        lax.fori_loop(1, cols, one, 0)

    nod = lambda c: w.own
    far_copies(start)
    row_copies(nod, w.q_nodes, qn_send, qn_recv, start)
    w.q_nodes[col] = w.own[...]

    @pl.when(own_key)
    def _():
        w.k_nodes[half * cols + col] = w.own[...]

    @pl.when(relay)
    def _():
        def forward(n, carry):
            pair = lax.rem(level + 1 + n, cols // 2)
            for side in range(2):
                c = 2 * pair + side

                @pl.when(jnp.logical_not(jnp.logical_and(own_key, c == col)))
                def _(c=c):
                    into = w.k_nodes.at[half * cols + c]
                    pltpu.make_async_copy(w.own, into, kz_recv.at[c]).wait()

            for step in range(1, 4):
                relay_copy(pair, step).start()
            return carry

        lax.fori_loop(0, cols // 2, forward, 0)

    wait_row(nod, w.q_nodes, qn_recv)
    for side in range(2):

        @pl.when(jnp.logical_not(jnp.logical_and(relay, half == side)))
        def _(side=side):
            def arrive(pair, carry):
                part = w.k_nodes.at[pl.ds(side * cols + 2 * pair, 2)]
                pltpu.make_async_copy(part, part, kx_recv.at[side * (cols // 2) + pair]).wait()
                return carry

            lax.fori_loop(0, cols // 2, arrive, 0)

    pair_distances(w)
    geometry(w)
    for load in loads[-2:]:
        load.wait()
    project(w)
    attention(w)
    att = lambda c: w.att_s.at[c]
    lse = lambda c: w.lse_s.at[c]
    dis = lambda c: w.dis_s.at[c]
    row_copies(att, w.att_r, at_send, at_recv, start)
    row_copies(lse, w.lse_r, ls_send, ls_recv, start)
    w.att_r[col] = w.att_s[col]
    w.lse_r[col] = w.lse_s[col]
    displacement(w)
    row_copies(dis, w.dis_r, ds_send, ds_recv, start)
    w.dis_r[col] = w.dis_s[col]
    far_copies(sent)
    row_copies(nod, w.q_nodes, qn_send, qn_recv, sent)

    @pl.when(relay)
    def _():
        def drain(n, carry):
            for step in range(1, 4):
                relay_copy(n, step).wait_send()
            return carry

        lax.fori_loop(0, cols // 2, drain, 0)

    row_copies(att, w.att_r, at_send, at_recv, sent)
    row_copies(lse, w.lse_r, ls_send, ls_recv, sent)
    wait_row(att, w.att_r, at_recv)
    wait_row(lse, w.lse_r, ls_recv)
    w.attended[...] = combine_attended(w)
    row_copies(dis, w.dis_r, ds_send, ds_recv, sent)
    wait_row(dis, w.dis_r, ds_recv)
    w.moved[...] = combine_moved(w)


def shards(
    nodes,
    coords,
    atom_types,
    segment_ids,
    pair_mask,
    pair_bias,
    ln_gain,
    w_qkv,
    gauss_mul,
    gauss_add,
    gauss_mean,
    gauss_width,
    w_gauss,
    w_heads,
    w_coord1,
    w_coord2,
    *,
    rows,
    cols,
):
    vmem = pl.BlockSpec(memory_space=pltpu.VMEM)
    hbm = pl.BlockSpec(memory_space=pl.ANY)
    dma = lambda n: pltpu.SemaphoreType.DMA((n,))
    return pl.pallas_call(
        functools.partial(kernel, rows, cols),
        out_shape=(
            jax.ShapeDtypeStruct(nodes.shape, BF16),
            jax.ShapeDtypeStruct(coords.shape, F32),
        ),
        in_specs=[hbm] * len(LOADED),
        out_specs=(vmem, vmem),
        scratch_shapes=[pltpu.VMEM(*spec) for spec in [*LOADED.values(), *WORK.values()]]
        + [dma(len(LOADED)), dma(rows // 4), dma(cols), dma(3 * cols // 2), dma(cols)]
        + [dma(cols)] * 8,
        compiler_params=pltpu.CompilerParams(collective_id=0, has_side_effects=True),
        name="refine",
    )(
        nodes,
        coords,
        atom_types[None],
        segment_ids[None],
        ln_gain[None],
        gauss_mean[None],
        gauss_width[None],
        w_gauss,
        w_coord1,
        w_coord2[None],
        gauss_mul,
        gauss_add,
        w_heads.T,
        pair_mask,
        w_qkv,
        pair_bias,
    )


def solution(mesh):
    in_specs = (
        P(("row", "col"), None),
        P(None, ("row", "col")),
        P(("row", "col")),
        P(("row", "col")),
        P("row", "col"),
        P(None, "row", "col"),
    ) + (P(),) * 10
    out_specs = (P(("row", "col"), None), P(None, ("row", "col")))
    body = functools.partial(shards, rows=mesh.shape["row"], cols=mesh.shape["col"])
    return jax.shard_map(body, mesh=mesh, in_specs=in_specs, out_specs=out_specs, check_vma=False)
```

```python
import functools
import math

import jax
import jax.numpy as jnp
from jax import lax
from jax.experimental import pallas as pl
from jax.experimental.pallas import tpu as pltpu
from jax.sharding import PartitionSpec as P

MESH = pl.DeviceIdType.MESH
F32 = jnp.float32
BF16 = jnp.bfloat16
ln_epsilon = 1e-05
masked_fill = -1000000000.0
root_shift = 0.01
GELU_A = math.sqrt(2.0 / math.pi)
GELU_B = GELU_A * 0.044715


def gelu(x):
    half = 0.5 * x
    return half + half * jnp.tanh(x * (GELU_A + GELU_B * (x * x)))


def nt_dot(a, b):
    return lax.dot_general(a, b, (((1,), (1,)), ((), ())), preferred_element_type=F32)


def nn_dot(a, b, precision=None):
    return jnp.dot(a, b, preferred_element_type=F32, precision=precision)


def lanes(shape):
    return lax.broadcasted_iota(jnp.int32, shape, len(shape) - 1)


def layer_norm(nodes, gain):
    x = nodes.astype(F32)
    centred = x - jnp.mean(x, axis=1, keepdims=True)
    spread = jnp.mean(centred * centred, axis=1, keepdims=True)
    return (centred * lax.rsqrt(spread + ln_epsilon) * gain).astype(BF16)


def prepare(w):
    w.wg_t[...] = w.w_gauss[...].astype(F32).T.astype(BF16)
    w.w1_t[...] = w.w_coord1[...].astype(F32).T.astype(BF16)
    w2 = w.w_coord2[...].astype(F32)
    wide = jnp.concatenate([w2] * 8, axis=1)
    own = lanes((8, 512)) // 64 == lax.broadcasted_iota(jnp.int32, (8, 512), 0)
    w.w2_b[...] = jnp.where(own, jnp.broadcast_to(wide, (8, 512)), 0.0).astype(BF16)
    mean = jnp.broadcast_to(w.gauss_mean[...], (128, 128)).T
    width = jnp.broadcast_to(w.gauss_width[...], (128, 128)).T
    slope = math.sqrt(0.5 * math.log2(math.e)) / width
    w.g_a[...] = slope
    w.g_b[...] = slope * mean
    w.g_c[...] = -jnp.log2(math.sqrt(2.0 * math.pi) * width)


def joined(parts):
    return parts + pltpu.roll(parts, 120, 1) + pltpu.roll(parts, 112, 1)


def pair_distances(w):
    for s in range(w.q_nodes.shape[0]):
        w.q_f[4 * s : 4 * s + 4, :] = w.q_nodes[s].astype(F32)
    for s in range(w.k_nodes.shape[0]):
        w.k_f[4 * s : 4 * s + 4, :] = w.k_nodes[s].astype(F32)
    qt = joined(w.q_f[:, 512:640])
    w.q_t[...] = qt
    kt = joined(w.k_f[:, 512:640]).T
    w.k_row[...] = kt[0:8, :]
    total = root_shift
    for axis in range(3):
        offset = qt[:, axis : axis + 1] - kt[axis : axis + 1, :]
        total = total + offset * offset
    distance = jnp.sqrt(total)
    kinds = w.gauss_mul.shape[0]
    q_hot = (lanes((64, kinds)).astype(F32) == qt[:, 3:4]).astype(F32)
    k_hot = (lax.broadcasted_iota(jnp.int32, (kinds, 128), 0).astype(F32) == kt[3:4, :]).astype(F32)
    high = lax.Precision.HIGHEST
    scale = nn_dot(nn_dot(q_hot, w.gauss_mul[...], high), k_hot, high)
    shift = nn_dot(nn_dot(q_hot, w.gauss_add[...], high), k_hot, high)
    w.expanded[...] = scale * distance + shift


def geometry(w, q, logits):
    a, b, k = w.g_a[...], w.g_b[...], w.g_c[...]
    for part in range(2):
        rows = w.expanded[pl.ds(pl.multiple_of(16 * q + 8 * part, 8), 8), :]
        pieces = []
        for i in range(8):
            t = a * rows[i : i + 1, :] - b
            pieces.append(jnp.exp2(k - t * t).astype(BF16))
        hidden = gelu(nn_dot(w.wg_t[...], jnp.concatenate(pieces, axis=1))).astype(BF16)
        geo = nn_dot(w.w_heads[...], hidden)
        for i in range(8):
            logits[pl.ds(8 * part + i, 64, stride=16), :] = geo[:, 128 * i : 128 * i + 128]


def project(w):
    qn = w.q_f[:, 0:512].astype(BF16)
    kn = w.k_f[:, 0:512].astype(BF16)
    w.q_p[...] = nn_dot(qn, w.w_qkv[:, 0:512]).astype(BF16)
    w.k_p[...] = nn_dot(kn, w.w_qkv[:, 512:1024]).astype(BF16)
    w.v_p[...] = nn_dot(kn, w.w_qkv[:, 1024:1536]).astype(BF16)


def attention(w, q, logits):
    here = pl.ds(pl.multiple_of(16 * q, 16), 16)
    take = (w.mask[here, :] == 1)[None]
    lane = lanes((16, 128))
    own = [(lane >> 3) == head for head in range(16)]
    ones = jnp.ones((128, 128), BF16)
    scale = 1.0 / math.sqrt(8.0)
    maxima = jnp.zeros((16, 128), F32)
    totals = jnp.ones((16, 128), F32)
    for g in range(4):
        cols = slice(128 * g, 128 * g + 128)
        rows = slice(256 * g, 256 * g + 256)
        q_g = w.q_p[here, cols].astype(F32)
        left = jnp.concatenate([jnp.where(o, q_g, 0.0).astype(BF16) for o in own], axis=0)
        bias = w.bias[16 * g : 16 * g + 16, here, :].astype(F32).reshape(256, 128)
        logit = bias + logits[rows, :] + nt_dot(left, w.k_p[:, cols]) * scale
        logits[rows, :] = logit
        masked = jnp.where(take, logit.reshape(16, 16, 128), masked_fill)
        top = jnp.max(masked, axis=2, keepdims=True)
        probs = jnp.exp(masked - top).astype(BF16).reshape(256, 128)
        out = nn_dot(probs, jnp.concatenate([w.v_p[:, cols], ones], axis=1))
        num = jnp.zeros((16, 128), F32)
        den = jnp.ones((16, 128), F32)
        for head in range(16):
            part = out[16 * head : 16 * head + 16]
            num = jnp.where(own[head], part[:, 0:128], num)
            den = jnp.where(own[head], part[:, 128:256], den)
            column = lane == 16 * g + head
            maxima = jnp.where(column, top[head], maxima)
            totals = jnp.where(column, part[:, 128:256], totals)
        part = num / den
        for s in range(4):
            w.att_s[4 * q + s, :, cols] = part[4 * s : 4 * s + 4].astype(BF16)
    return maxima + jnp.log(totals)


def displacement(w, q, logits, stat):
    here = pl.ds(pl.multiple_of(16 * q, 16), 16)
    pieces = []
    for part in range(2):
        parts = [logits[pl.ds(8 * part + i, 64, stride=16), :].astype(BF16) for i in range(8)]
        mixed = gelu(nn_dot(w.w1_t[...], jnp.concatenate(parts, axis=1))).astype(BF16)
        stacked = jnp.concatenate([mixed[:, 128 * i : 128 * i + 128] for i in range(8)], axis=0)
        pieces.append(nn_dot(w.w2_b[...], stacked))
    strength = jnp.where(w.mask[here, :] == 1, jnp.concatenate(pieces, axis=0), 0.0)
    qt = w.q_t[here, :]
    lane = lanes((16, 128))
    for axis in range(3):
        offset = qt[:, axis : axis + 1] - w.k_row[axis : axis + 1, :]
        moved = jnp.sum(strength * offset, axis=1, keepdims=True) * (1.0 / w.atoms)
        stat = jnp.where(lane == 64 + axis, moved, stat)
    for s in range(4):
        w.lse_s[4 * q + s] = stat[4 * s : 4 * s + 4]


def combine_attended(w):
    count = 16
    top = w.lse_r[0]
    for s in range(1, count):
        top = jnp.maximum(top, w.lse_r[s])
    total = jnp.zeros((4, 128), F32)
    for s in range(count):
        e = jnp.exp(w.lse_r[s] - top)
        w.coef[4 * s : 4 * s + 4, :] = e
        total = total + e
    inverse = 1.0 / total
    for s in range(count):
        w.coef[4 * s : 4 * s + 4, :] = w.coef[4 * s : 4 * s + 4, :] * inverse
    spread = (lanes((128, 512)) // 8 == lax.broadcasted_iota(jnp.int32, (128, 512), 0)).astype(BF16)
    coef = w.coef[...]
    top_part = coef.astype(BF16)
    rest = (coef - top_part.astype(F32)).astype(BF16)
    w.q_f[:, 0:512] = nn_dot(top_part, spread) + nn_dot(rest, spread)
    result = jnp.zeros((4, 512), F32)
    for s in range(count):
        result = result + w.q_f[4 * s : 4 * s + 4, 0:512] * w.att_r[s].astype(F32)
    return result.astype(BF16)


def combine_moved(w):
    total = w.lse_r[0]
    for s in range(1, 16):
        total = total + w.lse_r[s]
    w.pad[0:4, :] = total
    w.pad_t[...] = w.pad[...].T
    return w.coords[...] + w.pad_t[64:67, 0:4]


LOADED = dict(
    nodes=((4, 512), BF16),
    coords=((3, 4), F32),
    types=((1, 4), jnp.int32),
    segments=((1, 4), jnp.int32),
    ln_gain=((1, 512), F32),
    gauss_mean=((1, 128), F32),
    gauss_width=((1, 128), F32),
    w_gauss=((128, 128), BF16),
    w_coord1=((64, 64), BF16),
    w_coord2=((1, 64), BF16),
    gauss_mul=((60, 60), F32),
    gauss_add=((60, 60), F32),
    w_heads=((64, 128), BF16),
    mask=((64, 128), jnp.int32),
    w_qkv=((512, 1536), BF16),
    bias=((64, 64, 128), BF16),
)
WORK = dict(
    wg_t=((128, 128), BF16),
    w1_t=((64, 64), BF16),
    w2_b=((8, 512), BF16),
    g_a=((128, 128), F32),
    g_b=((128, 128), F32),
    g_c=((128, 128), F32),
    q_t=((64, 128), F32),
    k_row=((8, 128), F32),
    expanded=((64, 128), F32),
    logits=((4, 1024, 128), F32),
    q_f=((64, 640), F32),
    k_f=((128, 640), F32),
    q_p=((64, 512), BF16),
    k_p=((128, 512), BF16),
    v_p=((128, 512), BF16),
    coef=((64, 128), F32),
    pad=((128, 128), F32),
    pad_t=((128, 128), F32),
    own=((4, 640), BF16),
    q_nodes=((16, 4, 640), BF16),
    k_nodes=((32, 4, 640), BF16),
    att_s=((16, 4, 512), BF16),
    lse_s=((16, 4, 128), F32),
    att_r=((16, 4, 512), BF16),
    lse_r=((16, 4, 128), F32),
)


class Refs:
    pass


def own_block(w):
    w.own[:, 0:512] = layer_norm(w.nodes[...], w.ln_gain[...])
    w.pad[...] = jnp.zeros((128, 128), F32)
    rest = w.coords[...]
    for part in range(3):
        piece = rest.astype(BF16).astype(F32)
        w.pad[8 * part : 8 * part + 3, 0:4] = piece
        rest = rest - piece
    kinds = w.types[...] + w.gauss_mul.shape[0] // 2 * w.segments[...]
    w.pad[3:4, 0:4] = kinds.astype(F32)
    w.pad_t[...] = w.pad[...].T
    w.own[:, 512:640] = w.pad_t[0:4, :].astype(BF16)


def kernel(rows, cols, *refs):
    w = Refs()
    count = len(LOADED)
    sources, refs = refs[:count], refs[count:]
    w.attended, w.moved = refs[:2]
    refs = refs[2:]
    for name, ref in zip([*LOADED, *WORK], refs):
        setattr(w, name, ref)
    load_sem, kz_send, kz_recv, kx_send, kx_recv, qn_send, qn_recv = refs[-11:-4]
    at_send, at_recv, ls_send, ls_recv = refs[-4:]
    w.atoms = float(rows * cols * 4)
    row, col = lax.axis_index("row"), lax.axis_index("col")
    x, line = lax.rem(row, 4), lax.rem(row // 4, 2)
    level, core = col // 2, lax.rem(col, 2)
    home = row // 2
    own_key = home == col
    relay = core == x // 2
    half = lax.rem(x, 2)
    planes = rows // 4
    source_row = level * 4 + x

    def with_x(other):
        return row - x + other

    barrier = pltpu.get_barrier_semaphore()

    def greet(r, c):
        pl.semaphore_signal(barrier, inc=1, device_id=(r, c), device_id_type=MESH)

    def greet_row(n, carry):
        greet(row, lax.rem(col + n, cols))
        return carry

    @pl.when(relay)
    def _():
        def greet_source(n, carry):
            @pl.when(jnp.logical_not(jnp.logical_and(source_row == row, n == col)))
            def _():
                greet(source_row, n)

            return carry

        lax.fori_loop(0, cols, greet_source, 0)

    lax.fori_loop(1, cols, greet_row, 0)
    for side in range(2):
        other = 2 * core + side

        @pl.when(other != x)
        def _(other=other):
            greet(with_x(other), col)

    loads = []
    for n, (name, source) in enumerate(zip(LOADED, sources, strict=True)):
        loads.append(pltpu.make_async_copy(source, getattr(w, name), load_sem.at[n]))
        loads[-1].start()
    for load in loads[:5]:
        load.wait()
    own_block(w)

    pl.semaphore_wait(
        barrier, cols - 1 + planes - jnp.where(own_key, 1, 0) + jnp.where(relay, 3, 0)
    )

    def far_copy(n):
        plane = lax.rem(row // 4 + n, planes)
        return pltpu.make_async_remote_copy(
            src_ref=w.own,
            dst_ref=w.k_nodes.at[half * cols + col],
            send_sem=kz_send.at[n],
            recv_sem=kz_recv.at[col],
            device_id=(plane * 4 + x, home),
            device_id_type=MESH,
        )

    def far_copies(act):
        def one(n, carry):
            act(far_copy(n))
            return carry

        lax.fori_loop(1, planes, one, 0)

        @pl.when(jnp.logical_not(own_key))
        def _():
            act(far_copy(0))

    def relay_copy(pair, step):
        part = w.k_nodes.at[pl.ds(half * cols + 2 * pair, 2)]
        return pltpu.make_async_remote_copy(
            src_ref=part,
            dst_ref=part,
            send_sem=kx_send.at[pair * 3 + step - 1],
            recv_sem=kx_recv.at[half * (cols // 2) + pair],
            device_id=(with_x(lax.rem(x + step, 4)), col),
            device_id_type=MESH,
        )

    def row_copy(src, dst, send, recv, n):
        c = lax.rem(col + n, cols)
        return pltpu.make_async_remote_copy(
            src_ref=src(c),
            dst_ref=dst.at[col],
            send_sem=send.at[n],
            recv_sem=recv.at[col],
            device_id=(row, c),
            device_id_type=MESH,
        )

    def row_copies(src, dst, send, recv, act):
        def one(n, carry):
            act(row_copy(src, dst, send, recv, n))
            return carry

        lax.fori_loop(1, cols, one, 0)

    def start(copy):
        copy.start()

    def sent(copy):
        copy.wait_send()

    def wait_row(src, dst, recv):
        def one(n, carry):
            c = lax.rem(col + n, cols)
            pltpu.make_async_copy(src(c), dst.at[c], recv.at[c]).wait()
            return carry

        lax.fori_loop(1, cols, one, 0)

    nod = lambda c: w.own
    far_copies(start)
    row_copies(nod, w.q_nodes, qn_send, qn_recv, start)
    w.q_nodes[col] = w.own[...]

    @pl.when(own_key)
    def _():
        w.k_nodes[half * cols + col] = w.own[...]

    for load in loads[5:-2]:
        load.wait()
    prepare(w)

    @pl.when(relay)
    def _():
        def forward(n, carry):
            pair = lax.rem(level + 1 + n, cols // 2)
            for side in range(2):
                c = 2 * pair + side

                @pl.when(jnp.logical_not(jnp.logical_and(own_key, c == col)))
                def _(c=c):
                    into = w.k_nodes.at[half * cols + c]
                    pltpu.make_async_copy(w.own, into, kz_recv.at[c]).wait()

            for step in range(1, 4):
                relay_copy(pair, step).start()
            return carry

        lax.fori_loop(0, cols // 2, forward, 0)

    wait_row(nod, w.q_nodes, qn_recv)
    for side in range(2):

        @pl.when(jnp.logical_not(jnp.logical_and(relay, half == side)))
        def _(side=side):
            def arrive(pair, carry):
                part = w.k_nodes.at[pl.ds(side * cols + 2 * pair, 2)]
                pltpu.make_async_copy(part, part, kx_recv.at[side * (cols // 2) + pair]).wait()
                return carry

            lax.fori_loop(0, cols // 2, arrive, 0)

    pair_distances(w)
    for load in loads[-2:]:
        load.wait()
    project(w)

    def out_copy(src, dst, send, recv, c):
        return pltpu.make_async_remote_copy(
            src_ref=src.at[c],
            dst_ref=dst.at[col],
            send_sem=send.at[c],
            recv_sem=recv.at[col],
            device_id=(row, c),
            device_id_type=MESH,
        )

    def out_copies(q, src, dst, send, recv):
        for s in range(4):
            c = 4 * q + s

            @pl.when(c != col)
            def _(c=c):
                out_copy(src, dst, send, recv, c).start()

    mine = level // 2
    far = mine // 2
    for n, q in enumerate((3 - 3 * far, 2 - far, mine + 1 - 2 * lax.rem(mine, 2), mine)):
        logits = w.logits.at[n]
        geometry(w, q, logits)
        stat = attention(w, q, logits)
        out_copies(q, w.att_s, w.att_r, at_send, at_recv)
        displacement(w, q, logits, stat)
        out_copies(q, w.lse_s, w.lse_r, ls_send, ls_recv)
    w.att_r[col] = w.att_s[col]
    w.lse_r[col] = w.lse_s[col]
    far_copies(sent)
    row_copies(nod, w.q_nodes, qn_send, qn_recv, sent)

    @pl.when(relay)
    def _():
        def drain(n, carry):
            for step in range(1, 4):
                relay_copy(n, step).wait_send()
            return carry

        lax.fori_loop(0, cols // 2, drain, 0)

    def finish(n, carry):
        c = lax.rem(col + n, cols)
        for src, dst, send, recv in (
            (w.att_s, w.att_r, at_send, at_recv),
            (w.lse_s, w.lse_r, ls_send, ls_recv),
        ):
            out_copy(src, dst, send, recv, c).wait_send()
            pltpu.make_async_copy(src.at[c], dst.at[c], recv.at[c]).wait()
        return carry

    lax.fori_loop(1, cols, finish, 0)
    w.attended[...] = combine_attended(w)
    w.moved[...] = combine_moved(w)


def shards(
    nodes,
    coords,
    atom_types,
    segment_ids,
    pair_mask,
    pair_bias,
    ln_gain,
    w_qkv,
    gauss_mul,
    gauss_add,
    gauss_mean,
    gauss_width,
    w_gauss,
    w_heads,
    w_coord1,
    w_coord2,
    *,
    rows,
    cols,
):
    vmem = pl.BlockSpec(memory_space=pltpu.VMEM)
    hbm = pl.BlockSpec(memory_space=pl.ANY)
    dma = lambda n: pltpu.SemaphoreType.DMA((n,))
    return pl.pallas_call(
        functools.partial(kernel, rows, cols),
        out_shape=(
            jax.ShapeDtypeStruct(nodes.shape, BF16),
            jax.ShapeDtypeStruct(coords.shape, F32),
        ),
        in_specs=[hbm] * len(LOADED),
        out_specs=(vmem, vmem),
        scratch_shapes=[pltpu.VMEM(*spec) for spec in [*LOADED.values(), *WORK.values()]]
        + [dma(len(LOADED)), dma(rows // 4), dma(cols), dma(3 * cols // 2), dma(cols)]
        + [dma(cols)] * 6,
        compiler_params=pltpu.CompilerParams(collective_id=0, has_side_effects=True),
        name="refine",
    )(
        nodes,
        coords,
        atom_types[None],
        segment_ids[None],
        ln_gain[None],
        gauss_mean[None],
        gauss_width[None],
        w_gauss,
        w_coord1,
        w_coord2[None],
        gauss_mul,
        gauss_add,
        w_heads.T,
        pair_mask,
        w_qkv,
        pair_bias,
    )


def solution(mesh):
    in_specs = (
        P(("row", "col"), None),
        P(None, ("row", "col")),
        P(("row", "col")),
        P(("row", "col")),
        P("row", "col"),
        P(None, "row", "col"),
    ) + (P(),) * 10
    out_specs = (P(("row", "col"), None), P(None, ("row", "col")))
    body = functools.partial(shards, rows=mesh.shape["row"], cols=mesh.shape["col"])
    return jax.shard_map(body, mesh=mesh, in_specs=in_specs, out_specs=out_specs, check_vma=False)
```

```python
import functools
import math

import jax
import jax.numpy as jnp
from jax import lax
from jax.experimental import pallas as pl
from jax.experimental.pallas import tpu as pltpu
from jax.sharding import PartitionSpec as P

MESH = pl.DeviceIdType.MESH
F32 = jnp.float32
BF16 = jnp.bfloat16
ln_epsilon = 1e-05
masked_fill = -1000000000.0
root_shift = 0.01
GELU_A = math.sqrt(2.0 / math.pi)
GELU_B = GELU_A * 0.044715


def gelu(x):
    half = 0.5 * x
    return half + half * jnp.tanh(x * (GELU_A + GELU_B * (x * x)))


def nt_dot(a, b):
    return lax.dot_general(a, b, (((1,), (1,)), ((), ())), preferred_element_type=F32)


def nn_dot(a, b, precision=None):
    return jnp.dot(a, b, preferred_element_type=F32, precision=precision)


def lanes(shape):
    return lax.broadcasted_iota(jnp.int32, shape, len(shape) - 1)


def layer_norm(nodes, gain):
    x = nodes.astype(F32)
    centred = x - jnp.mean(x, axis=1, keepdims=True)
    spread = jnp.mean(centred * centred, axis=1, keepdims=True)
    return (centred * lax.rsqrt(spread + ln_epsilon) * gain).astype(BF16)


def prepare(w):
    w.wg_t[...] = w.w_gauss[...].astype(F32).T.astype(BF16)
    w.w1_t[...] = w.w_coord1[...].astype(F32).T.astype(BF16)
    w2 = w.w_coord2[...].astype(F32)
    wide = jnp.concatenate([w2] * 8, axis=1)
    own = lanes((8, 512)) // 64 == lax.broadcasted_iota(jnp.int32, (8, 512), 0)
    w.w2_b[...] = jnp.where(own, jnp.broadcast_to(wide, (8, 512)), 0.0).astype(BF16)
    mean = jnp.broadcast_to(w.gauss_mean[...], (128, 128)).T
    width = jnp.broadcast_to(w.gauss_width[...], (128, 128)).T
    slope = math.sqrt(0.5 * math.log2(math.e)) / width
    w.g_a[...] = slope
    w.g_b[...] = slope * mean
    w.g_c[...] = -jnp.log2(math.sqrt(2.0 * math.pi) * width)


def joined(parts):
    return parts + pltpu.roll(parts, 120, 1) + pltpu.roll(parts, 112, 1)


def pair_distances(w):
    for s in range(w.q_nodes.shape[0]):
        w.q_f[4 * s : 4 * s + 4, :] = w.q_nodes[s].astype(F32)
    for s in range(w.k_nodes.shape[0]):
        w.k_f[4 * s : 4 * s + 4, :] = w.k_nodes[s].astype(F32)
    qt = joined(w.q_f[:, 512:640])
    w.q_t[...] = qt
    kt = joined(w.k_f[:, 512:640]).T
    w.k_row[...] = kt[0:8, :]
    total = root_shift
    for axis in range(3):
        offset = qt[:, axis : axis + 1] - kt[axis : axis + 1, :]
        total = total + offset * offset
    distance = jnp.sqrt(total)
    kinds = w.gauss_mul.shape[0]
    q_hot = (lanes((64, kinds)).astype(F32) == qt[:, 3:4]).astype(F32)
    k_hot = (lax.broadcasted_iota(jnp.int32, (kinds, 128), 0).astype(F32) == kt[3:4, :]).astype(F32)
    high = lax.Precision.HIGHEST
    scale = nn_dot(nn_dot(q_hot, w.gauss_mul[...], high), k_hot, high)
    shift = nn_dot(nn_dot(q_hot, w.gauss_add[...], high), k_hot, high)
    w.expanded[...] = scale * distance + shift


def geometry(w, q, logits):
    a, b, k = w.g_a[...], w.g_b[...], w.g_c[...]
    for part in range(2):
        rows = w.expanded[pl.ds(pl.multiple_of(16 * q + 8 * part, 8), 8), :]
        pieces = []
        for i in range(8):
            t = a * rows[i : i + 1, :] - b
            pieces.append(jnp.exp2(k - t * t).astype(BF16))
        hidden = gelu(nn_dot(w.wg_t[...], jnp.concatenate(pieces, axis=1))).astype(BF16)
        geo = nn_dot(w.w_heads[...], hidden)
        for i in range(8):
            logits[pl.ds(8 * part + i, 64, stride=16), :] = geo[:, 128 * i : 128 * i + 128]


def project(w):
    qn = w.q_f[:, 0:512].astype(BF16)
    kn = w.k_f[:, 0:512].astype(BF16)
    w.q_p[...] = nn_dot(qn, w.w_qkv[:, 0:512]).astype(BF16)
    w.k_p[...] = nn_dot(kn, w.w_qkv[:, 512:1024]).astype(BF16)
    w.v_p[...] = nn_dot(kn, w.w_qkv[:, 1024:1536]).astype(BF16)


def attention(w, q, logits):
    here = pl.ds(pl.multiple_of(16 * q, 16), 16)
    take = (w.mask[here, :] == 1)[None]
    lane = lanes((16, 128))
    own = [(lane >> 3) == head for head in range(16)]
    ones = jnp.ones((128, 128), BF16)
    scale = 1.0 / math.sqrt(8.0)
    maxima = jnp.zeros((16, 128), F32)
    totals = jnp.ones((16, 128), F32)
    for g in range(4):
        cols = slice(128 * g, 128 * g + 128)
        rows = slice(256 * g, 256 * g + 256)
        q_g = w.q_p[here, cols].astype(F32)
        left = jnp.concatenate([jnp.where(o, q_g, 0.0).astype(BF16) for o in own], axis=0)
        bias = w.bias[16 * g : 16 * g + 16, here, :].astype(F32).reshape(256, 128)
        logit = bias + logits[rows, :] + nt_dot(left, w.k_p[:, cols]) * scale
        logits[rows, :] = logit
        masked = jnp.where(take, logit.reshape(16, 16, 128), masked_fill)
        top = jnp.max(masked, axis=2, keepdims=True)
        probs = jnp.exp(masked - top).astype(BF16).reshape(256, 128)
        out = nn_dot(probs, jnp.concatenate([w.v_p[:, cols], ones], axis=1))
        num = jnp.zeros((16, 128), F32)
        den = jnp.ones((16, 128), F32)
        for head in range(16):
            part = out[16 * head : 16 * head + 16]
            num = jnp.where(own[head], part[:, 0:128], num)
            den = jnp.where(own[head], part[:, 128:256], den)
            column = lane == 16 * g + head
            maxima = jnp.where(column, top[head], maxima)
            totals = jnp.where(column, part[:, 128:256], totals)
        part = num / den
        for s in range(4):
            w.att_s[4 * q + s, :, cols] = part[4 * s : 4 * s + 4].astype(BF16)
    return maxima + jnp.log(totals)


def displacement(w, q, logits, stat):
    here = pl.ds(pl.multiple_of(16 * q, 16), 16)
    pieces = []
    for part in range(2):
        parts = [logits[pl.ds(8 * part + i, 64, stride=16), :].astype(BF16) for i in range(8)]
        mixed = gelu(nn_dot(w.w1_t[...], jnp.concatenate(parts, axis=1))).astype(BF16)
        stacked = jnp.concatenate([mixed[:, 128 * i : 128 * i + 128] for i in range(8)], axis=0)
        pieces.append(nn_dot(w.w2_b[...], stacked))
    strength = jnp.where(w.mask[here, :] == 1, jnp.concatenate(pieces, axis=0), 0.0)
    qt = w.q_t[here, :]
    lane = lanes((16, 128))
    for axis in range(3):
        offset = qt[:, axis : axis + 1] - w.k_row[axis : axis + 1, :]
        moved = jnp.sum(strength * offset, axis=1, keepdims=True) * (1.0 / w.atoms)
        stat = jnp.where(lane == 64 + axis, moved, stat)
    for s in range(4):
        w.lse_s[4 * q + s] = stat[4 * s : 4 * s + 4]


def combine_attended(w):
    count = 16
    top = w.lse_r[0]
    for s in range(1, count):
        top = jnp.maximum(top, w.lse_r[s])
    total = jnp.zeros((4, 128), F32)
    for s in range(count):
        e = jnp.exp(w.lse_r[s] - top)
        w.coef[4 * s : 4 * s + 4, :] = e
        total = total + e
    inverse = 1.0 / total
    for s in range(count):
        w.coef[4 * s : 4 * s + 4, :] = w.coef[4 * s : 4 * s + 4, :] * inverse
    spread = (lanes((128, 512)) // 8 == lax.broadcasted_iota(jnp.int32, (128, 512), 0)).astype(BF16)
    coef = w.coef[...]
    top_part = coef.astype(BF16)
    rest = (coef - top_part.astype(F32)).astype(BF16)
    w.q_f[:, 0:512] = nn_dot(top_part, spread) + nn_dot(rest, spread)
    result = jnp.zeros((4, 512), F32)
    for s in range(count):
        result = result + w.q_f[4 * s : 4 * s + 4, 0:512] * w.att_r[s].astype(F32)
    return result.astype(BF16)


def combine_moved(w):
    total = w.lse_r[0]
    for s in range(1, 16):
        total = total + w.lse_r[s]
    w.pad[0:4, :] = total
    w.pad_t[...] = w.pad[...].T
    return w.coords[...] + w.pad_t[64:67, 0:4]


LOADED = dict(
    nodes=((4, 512), BF16),
    coords=((3, 4), F32),
    types=((1, 4), jnp.int32),
    segments=((1, 4), jnp.int32),
    ln_gain=((1, 512), F32),
    gauss_mean=((1, 128), F32),
    gauss_width=((1, 128), F32),
    w_gauss=((128, 128), BF16),
    w_coord1=((64, 64), BF16),
    w_coord2=((1, 64), BF16),
    gauss_mul=((60, 60), F32),
    gauss_add=((60, 60), F32),
    w_heads=((64, 128), BF16),
    mask=((64, 128), jnp.int32),
    w_qkv=((512, 1536), BF16),
    bias=((64, 64, 128), BF16),
)
WORK = dict(
    wg_t=((128, 128), BF16),
    w1_t=((64, 64), BF16),
    w2_b=((8, 512), BF16),
    g_a=((128, 128), F32),
    g_b=((128, 128), F32),
    g_c=((128, 128), F32),
    q_t=((64, 128), F32),
    k_row=((8, 128), F32),
    expanded=((64, 128), F32),
    logits=((4, 1024, 128), F32),
    q_f=((64, 640), F32),
    k_f=((128, 640), F32),
    q_p=((64, 512), BF16),
    k_p=((128, 512), BF16),
    v_p=((128, 512), BF16),
    coef=((64, 128), F32),
    pad=((128, 128), F32),
    pad_t=((128, 128), F32),
    own=((4, 640), BF16),
    q_nodes=((16, 4, 640), BF16),
    k_nodes=((32, 4, 640), BF16),
    att_s=((16, 4, 512), BF16),
    lse_s=((16, 4, 128), F32),
    att_r=((16, 4, 512), BF16),
    lse_r=((16, 4, 128), F32),
)


class Refs:
    pass


def own_block(w):
    w.own[:, 0:512] = layer_norm(w.nodes[...], w.ln_gain[...])
    w.pad[...] = jnp.zeros((128, 128), F32)
    rest = w.coords[...]
    for part in range(3):
        piece = rest.astype(BF16).astype(F32)
        w.pad[8 * part : 8 * part + 3, 0:4] = piece
        rest = rest - piece
    kinds = w.types[...] + w.gauss_mul.shape[0] // 2 * w.segments[...]
    w.pad[3:4, 0:4] = kinds.astype(F32)
    w.pad_t[...] = w.pad[...].T
    w.own[:, 512:640] = w.pad_t[0:4, :].astype(BF16)


def kernel(rows, cols, *refs):
    w = Refs()
    count = len(LOADED)
    sources, refs = refs[:count], refs[count:]
    w.attended, w.moved = refs[:2]
    refs = refs[2:]
    for name, ref in zip([*LOADED, *WORK], refs):
        setattr(w, name, ref)
    load_sem, kz_send, kz_recv, kx_send, kx_recv, qn_send, qn_recv = refs[-11:-4]
    at_send, at_recv, ls_send, ls_recv = refs[-4:]
    w.atoms = float(rows * cols * 4)
    row, col = lax.axis_index("row"), lax.axis_index("col")
    x, line = lax.rem(row, 4), lax.rem(row // 4, 2)
    level, core = col // 2, lax.rem(col, 2)
    home = row // 2
    own_key = home == col
    relay = core == x // 2
    half = lax.rem(x, 2)
    planes = rows // 4
    source_row = level * 4 + x

    def with_x(other):
        return row - x + other

    barrier = pltpu.get_barrier_semaphore()

    def greet(r, c):
        pl.semaphore_signal(barrier, inc=1, device_id=(r, c), device_id_type=MESH)

    def greet_row(n, carry):
        greet(row, lax.rem(col + n, cols))
        return carry

    @pl.when(relay)
    def _():
        def greet_source(n, carry):
            @pl.when(jnp.logical_not(jnp.logical_and(source_row == row, n == col)))
            def _():
                greet(source_row, n)

            return carry

        lax.fori_loop(0, cols, greet_source, 0)

    lax.fori_loop(1, cols, greet_row, 0)
    for side in range(2):
        other = 2 * core + side

        @pl.when(other != x)
        def _(other=other):
            greet(with_x(other), col)

    loads = []
    for n, (name, source) in enumerate(zip(LOADED, sources, strict=True)):
        loads.append(pltpu.make_async_copy(source, getattr(w, name), load_sem.at[n]))
        loads[-1].start()
    for load in loads[:5]:
        load.wait()
    own_block(w)

    pl.semaphore_wait(
        barrier, cols - 1 + planes - jnp.where(own_key, 1, 0) + jnp.where(relay, 3, 0)
    )

    def far_copy(n):
        plane = lax.rem(row // 4 + n, planes)
        return pltpu.make_async_remote_copy(
            src_ref=w.own,
            dst_ref=w.k_nodes.at[half * cols + col],
            send_sem=kz_send.at[n],
            recv_sem=kz_recv.at[col],
            device_id=(plane * 4 + x, home),
            device_id_type=MESH,
        )

    def far_copies(act):
        for n in [*range(planes // 2 + 1, 0, -2), *range(planes - 1, planes // 2 + 1, -2)]:
            act(far_copy(n))
        for n in range(planes // 2, 0, -2):
            act(far_copy(n))
        for n in range(planes - 2, planes // 2, -2):
            act(far_copy(n))

        @pl.when(jnp.logical_not(own_key))
        def _():
            act(far_copy(0))

    def relay_copy(pair, step):
        part = w.k_nodes.at[pl.ds(half * cols + 2 * pair, 2)]
        return pltpu.make_async_remote_copy(
            src_ref=part,
            dst_ref=part,
            send_sem=kx_send.at[pair * 3 + step - 1],
            recv_sem=kx_recv.at[half * (cols // 2) + pair],
            device_id=(with_x(lax.rem(x + step, 4)), col),
            device_id_type=MESH,
        )

    def row_copy(src, dst, send, recv, n):
        c = lax.rem(col + cols - n, cols)
        return pltpu.make_async_remote_copy(
            src_ref=src(c),
            dst_ref=dst.at[col],
            send_sem=send.at[n],
            recv_sem=recv.at[col],
            device_id=(row, c),
            device_id_type=MESH,
        )

    def row_copies(src, dst, send, recv, act):
        def one(n, carry):
            act(row_copy(src, dst, send, recv, n))
            return carry

        lax.fori_loop(1, cols, one, 0)

    def start(copy):
        copy.start()

    def sent(copy):
        copy.wait_send()

    def wait_row(src, dst, recv):
        def one(n, carry):
            c = lax.rem(col + n, cols)
            pltpu.make_async_copy(src(c), dst.at[c], recv.at[c]).wait()
            return carry

        lax.fori_loop(1, cols, one, 0)

    nod = lambda c: w.own
    far_copies(start)
    row_copies(nod, w.q_nodes, qn_send, qn_recv, start)
    w.q_nodes[col] = w.own[...]

    @pl.when(own_key)
    def _():
        w.k_nodes[half * cols + col] = w.own[...]

    for load in loads[5:-2]:
        load.wait()
    prepare(w)

    @pl.when(relay)
    def _():
        def forward(n, carry):
            m = jnp.where(line == lax.rem(level, 2), n, cols // 2 - 1 - n)
            shift = (m + 1) // 2 * (2 * lax.rem(m, 2) - 1)
            pair = lax.rem(level + shift + cols // 2, cols // 2)
            for side in range(2):
                c = 2 * pair + side

                @pl.when(jnp.logical_not(jnp.logical_and(own_key, c == col)))
                def _(c=c):
                    into = w.k_nodes.at[half * cols + c]
                    pltpu.make_async_copy(w.own, into, kz_recv.at[c]).wait()

            for step in range(1, 4):
                relay_copy(pair, step).start()
            return carry

        lax.fori_loop(0, cols // 2, forward, 0)

    wait_row(nod, w.q_nodes, qn_recv)
    for side in range(2):

        @pl.when(jnp.logical_not(jnp.logical_and(relay, half == side)))
        def _(side=side):
            def arrive(pair, carry):
                part = w.k_nodes.at[pl.ds(side * cols + 2 * pair, 2)]
                pltpu.make_async_copy(part, part, kx_recv.at[side * (cols // 2) + pair]).wait()
                return carry

            lax.fori_loop(0, cols // 2, arrive, 0)

    pair_distances(w)
    for load in loads[-2:]:
        load.wait()
    project(w)

    def out_copy(src, dst, send, recv, c):
        return pltpu.make_async_remote_copy(
            src_ref=src.at[c],
            dst_ref=dst.at[col],
            send_sem=send.at[c],
            recv_sem=recv.at[col],
            device_id=(row, c),
            device_id_type=MESH,
        )

    def out_copies(q, src, dst, send, recv):
        for s in range(4):
            c = 4 * q + s

            @pl.when(c != col)
            def _(c=c):
                out_copy(src, dst, send, recv, c).start()

    mine = level // 2
    far = mine // 2
    for n, q in enumerate((3 - 3 * far, 2 - far, mine + 1 - 2 * lax.rem(mine, 2), mine)):
        logits = w.logits.at[n]
        geometry(w, q, logits)
        stat = attention(w, q, logits)
        out_copies(q, w.att_s, w.att_r, at_send, at_recv)
        displacement(w, q, logits, stat)
        out_copies(q, w.lse_s, w.lse_r, ls_send, ls_recv)
    w.att_r[col] = w.att_s[col]
    w.lse_r[col] = w.lse_s[col]
    far_copies(sent)
    row_copies(nod, w.q_nodes, qn_send, qn_recv, sent)

    @pl.when(relay)
    def _():
        def drain(n, carry):
            for step in range(1, 4):
                relay_copy(n, step).wait_send()
            return carry

        lax.fori_loop(0, cols // 2, drain, 0)

    def finish(n, carry):
        c = lax.rem(col + n, cols)
        for src, dst, send, recv in (
            (w.att_s, w.att_r, at_send, at_recv),
            (w.lse_s, w.lse_r, ls_send, ls_recv),
        ):
            out_copy(src, dst, send, recv, c).wait_send()
            pltpu.make_async_copy(src.at[c], dst.at[c], recv.at[c]).wait()
        return carry

    lax.fori_loop(1, cols, finish, 0)
    w.attended[...] = combine_attended(w)
    w.moved[...] = combine_moved(w)


def hand_over(attended_from, moved_from, attended, moved):
    attended[...] = attended_from[...]
    moved[...] = moved_from[...]


def shards(
    nodes,
    coords,
    atom_types,
    segment_ids,
    pair_mask,
    pair_bias,
    ln_gain,
    w_qkv,
    gauss_mul,
    gauss_add,
    gauss_mean,
    gauss_width,
    w_gauss,
    w_heads,
    w_coord1,
    w_coord2,
    *,
    rows,
    cols,
):
    vmem = pl.BlockSpec(memory_space=pltpu.VMEM)
    hbm = pl.BlockSpec(memory_space=pl.ANY)
    dma = lambda n: pltpu.SemaphoreType.DMA((n,))
    outs = (
        jax.ShapeDtypeStruct(nodes.shape, BF16),
        jax.ShapeDtypeStruct(coords.shape, F32),
    )
    results = pl.pallas_call(
        functools.partial(kernel, rows, cols),
        out_shape=outs,
        in_specs=[hbm] * len(LOADED),
        out_specs=(vmem, vmem),
        scratch_shapes=[pltpu.VMEM(*spec) for spec in [*LOADED.values(), *WORK.values()]]
        + [dma(len(LOADED)), dma(rows // 4), dma(cols), dma(3 * cols // 2), dma(cols)]
        + [dma(cols)] * 6,
        compiler_params=pltpu.CompilerParams(collective_id=0, has_side_effects=True),
        name="refine",
    )(
        nodes,
        coords,
        atom_types[None],
        segment_ids[None],
        ln_gain[None],
        gauss_mean[None],
        gauss_width[None],
        w_gauss,
        w_coord1,
        w_coord2[None],
        gauss_mul,
        gauss_add,
        w_heads.T,
        pair_mask,
        w_qkv,
        pair_bias,
    )
    return pl.pallas_call(
        hand_over,
        out_shape=outs,
        in_specs=[vmem, vmem],
        out_specs=(vmem, vmem),
        name="hand_over",
    )(*results)


def solution(mesh):
    in_specs = (
        P(("row", "col"), None),
        P(None, ("row", "col")),
        P(("row", "col")),
        P(("row", "col")),
        P("row", "col"),
        P(None, "row", "col"),
    ) + (P(),) * 10
    out_specs = (P(("row", "col"), None), P(None, ("row", "col")))
    body = functools.partial(shards, rows=mesh.shape["row"], cols=mesh.shape["col"])
    return jax.shard_map(body, mesh=mesh, in_specs=in_specs, out_specs=out_specs, check_vma=False)
```

```python
import functools
import math

import jax
import jax.numpy as jnp
from jax import lax
from jax.experimental import pallas as pl
from jax.experimental.pallas import tpu as pltpu
from jax.sharding import PartitionSpec as P

MESH = pl.DeviceIdType.MESH
F32 = jnp.float32
BF16 = jnp.bfloat16
ln_epsilon = 1e-05
masked_fill = -1000000000.0
root_shift = 0.01
GELU_A = math.sqrt(2.0 / math.pi)
GELU_B = GELU_A * 0.044715


def gelu(x):
    x = x.astype(BF16)
    half = x * BF16(0.5)
    return half + half * jnp.tanh(x * (BF16(GELU_A) + BF16(GELU_B) * (x * x)))


def nt_dot(a, b):
    return lax.dot_general(a, b, (((1,), (1,)), ((), ())), preferred_element_type=F32)


def nn_dot(a, b, precision=None):
    return jnp.dot(a, b, preferred_element_type=F32, precision=precision)


def lanes(shape):
    return lax.broadcasted_iota(jnp.int32, shape, len(shape) - 1)


def layer_norm(nodes, gain):
    x = nodes.astype(F32)
    centred = x - jnp.mean(x, axis=1, keepdims=True)
    spread = jnp.mean(centred * centred, axis=1, keepdims=True)
    return (centred * lax.rsqrt(spread + ln_epsilon) * gain).astype(BF16)


def prepare(w):
    w.wg_t[...] = w.w_gauss[...].astype(F32).T.astype(BF16)
    w.w1_t[...] = w.w_coord1[...].astype(F32).T.astype(BF16)
    w2 = w.w_coord2[...].astype(F32)
    wide = jnp.concatenate([w2] * 8, axis=1)
    own = lanes((8, 512)) // 64 == lax.broadcasted_iota(jnp.int32, (8, 512), 0)
    w.w2_b[...] = jnp.where(own, jnp.broadcast_to(wide, (8, 512)), 0.0).astype(BF16)
    mean = jnp.broadcast_to(w.gauss_mean[...], (128, 128)).T
    width = jnp.broadcast_to(w.gauss_width[...], (128, 128)).T
    slope = math.sqrt(0.5) / width
    w.g_a[...] = slope
    w.g_b[...] = slope * mean
    w.g_c[...] = -jnp.log(math.sqrt(2.0 * math.pi) * width)


def joined(parts):
    return parts + pltpu.roll(parts, 120, 1) + pltpu.roll(parts, 112, 1)


def query_side(w):
    for s in range(w.q_nodes.shape[0]):
        w.q_f[4 * s : 4 * s + 4, :] = w.q_nodes[s].astype(F32)
    w.q_p[...] = nn_dot(w.q_f[:, 0:512].astype(BF16), w.w_qkv[:, 0:512]).astype(BF16)
    qt = joined(w.q_f[:, 512:640])
    w.q_t[...] = qt
    kinds = w.gauss_mul.shape[0]
    q_hot = (lanes((64, kinds)).astype(F32) == qt[:, 3:4]).astype(F32)
    high = lax.Precision.HIGHEST
    w.q_mul[...] = nn_dot(q_hot, w.gauss_mul[...], high)
    w.q_add[...] = nn_dot(q_hot, w.gauss_add[...], high)


def pair_distances(w):
    for s in range(w.k_nodes.shape[0]):
        w.k_f[4 * s : 4 * s + 4, :] = w.k_nodes[s].astype(F32)
    qt = w.q_t[...]
    kt = joined(w.k_f[:, 512:640]).T
    w.k_row[...] = kt[0:8, :]
    total = root_shift
    for axis in range(3):
        offset = qt[:, axis : axis + 1] - kt[axis : axis + 1, :]
        total = total + offset * offset
    distance = jnp.sqrt(total)
    kinds = w.gauss_mul.shape[0]
    k_hot = (lax.broadcasted_iota(jnp.int32, (kinds, 128), 0).astype(F32) == kt[3:4, :]).astype(F32)
    high = lax.Precision.HIGHEST
    scale = nn_dot(w.q_mul[...], k_hot, high)
    shift = nn_dot(w.q_add[...], k_hot, high)
    w.expanded[...] = scale * distance + shift


def geometry(w, q, logits):
    a, b, k = w.g_a[...], w.g_b[...], w.g_c[...]
    for part in range(2):
        rows = w.expanded[pl.ds(pl.multiple_of(16 * q + 8 * part, 8), 8), :]
        pieces = []
        for i in range(8):
            t = a * rows[i : i + 1, :] - b
            pieces.append(jnp.exp(k - t * t).astype(BF16))
        hidden = gelu(nn_dot(w.wg_t[...], jnp.concatenate(pieces, axis=1)))
        geo = nn_dot(w.w_heads[...], hidden)
        for i in range(8):
            logits[pl.ds(8 * part + i, 64, stride=16), :] = geo[:, 128 * i : 128 * i + 128]


def project(w):
    kn = w.k_f[:, 0:512].astype(BF16)
    w.k_p[...] = nn_dot(kn, w.w_qkv[:, 512:1024]).astype(BF16)
    w.v_p[...] = nn_dot(kn, w.w_qkv[:, 1024:1536]).astype(BF16)


def attention(w, q, logits):
    here = pl.ds(pl.multiple_of(16 * q, 16), 16)
    take = (w.mask[here, :] == 1)[None]
    lane = lanes((16, 128))
    own = [(lane >> 3) == head for head in range(16)]
    keep = [jnp.where(o, 1.0, 0.0).astype(BF16) for o in own]
    ones = jnp.ones((128, 128), BF16)
    scale = 1.0 / math.sqrt(8.0)
    maxima = jnp.zeros((16, 128), F32)
    totals = jnp.ones((16, 128), F32)
    for g in range(4):
        cols = slice(128 * g, 128 * g + 128)
        rows = slice(256 * g, 256 * g + 256)
        q_g = w.q_p[here, cols]
        left = jnp.concatenate([q_g * k for k in keep], axis=0)
        bias = w.bias[16 * g : 16 * g + 16, here, :].astype(F32).reshape(256, 128)
        logit = bias + logits[rows, :] + nt_dot(left, w.k_p[:, cols]) * scale
        logits[rows, :] = logit
        masked = jnp.where(take, logit.reshape(16, 16, 128), masked_fill)
        top = jnp.max(masked, axis=2, keepdims=True)
        probs = jnp.exp(masked - top).astype(BF16).reshape(256, 128)
        out = nn_dot(probs, jnp.concatenate([w.v_p[:, cols], ones], axis=1))
        num = jnp.zeros((16, 128), F32)
        den = jnp.ones((16, 128), F32)
        for head in range(16):
            part = out[16 * head : 16 * head + 16]
            num = jnp.where(own[head], part[:, 0:128], num)
            den = jnp.where(own[head], part[:, 128:256], den)
            column = lane == 16 * g + head
            maxima = jnp.where(column, top[head], maxima)
            totals = jnp.where(column, part[:, 128:256], totals)
        part = num / den
        for s in range(4):
            w.att_s[4 * q + s, :, cols] = part[4 * s : 4 * s + 4].astype(BF16)
    return maxima + jnp.log(totals)


def displacement(w, q, logits, stat):
    here = pl.ds(pl.multiple_of(16 * q, 16), 16)
    pieces = []
    for part in range(2):
        parts = [logits[pl.ds(8 * part + i, 64, stride=16), :].astype(BF16) for i in range(8)]
        mixed = gelu(nn_dot(w.w1_t[...], jnp.concatenate(parts, axis=1)))
        stacked = jnp.concatenate([mixed[:, 128 * i : 128 * i + 128] for i in range(8)], axis=0)
        pieces.append(nn_dot(w.w2_b[...], stacked))
    strength = jnp.where(w.mask[here, :] == 1, jnp.concatenate(pieces, axis=0), 0.0)
    qt = w.q_t[here, :]
    lane = lanes((16, 128))
    for axis in range(3):
        offset = qt[:, axis : axis + 1] - w.k_row[axis : axis + 1, :]
        moved = jnp.sum(strength * offset, axis=1, keepdims=True) * (1.0 / w.atoms)
        stat = jnp.where(lane == 64 + axis, moved, stat)
    for s in range(4):
        w.lse_s[4 * q + s] = stat[4 * s : 4 * s + 4]


def combine_attended(w):
    count = 16
    top = w.lse_r[0]
    for s in range(1, count):
        top = jnp.maximum(top, w.lse_r[s])
    total = jnp.zeros((4, 128), F32)
    for s in range(count):
        e = jnp.exp(w.lse_r[s] - top)
        w.coef[4 * s : 4 * s + 4, :] = e
        total = total + e
    inverse = 1.0 / total
    for s in range(count):
        w.coef[4 * s : 4 * s + 4, :] = w.coef[4 * s : 4 * s + 4, :] * inverse
    spread = (lanes((128, 512)) // 8 == lax.broadcasted_iota(jnp.int32, (128, 512), 0)).astype(BF16)
    coef = w.coef[...]
    top_part = coef.astype(BF16)
    rest = (coef - top_part.astype(F32)).astype(BF16)
    w.q_f[:, 0:512] = nn_dot(top_part, spread) + nn_dot(rest, spread)
    result = jnp.zeros((4, 512), F32)
    for s in range(count):
        result = result + w.q_f[4 * s : 4 * s + 4, 0:512] * w.att_r[s].astype(F32)
    return result.astype(BF16)


def combine_moved(w):
    total = w.lse_r[0]
    for s in range(1, 16):
        total = total + w.lse_r[s]
    w.pad[0:4, :] = total
    w.pad_t[...] = w.pad[...].T
    return w.coords[...] + w.pad_t[64:67, 0:4]


LOADED = dict(
    nodes=((4, 512), BF16),
    coords=((3, 4), F32),
    types=((1, 4), jnp.int32),
    segments=((1, 4), jnp.int32),
    ln_gain=((1, 512), F32),
    gauss_mean=((1, 128), F32),
    gauss_width=((1, 128), F32),
    w_gauss=((128, 128), BF16),
    w_coord1=((64, 64), BF16),
    w_coord2=((1, 64), BF16),
    gauss_mul=((60, 60), F32),
    gauss_add=((60, 60), F32),
    w_heads=((64, 128), BF16),
    mask=((64, 128), jnp.int32),
    w_qkv=((512, 1536), BF16),
    bias=((64, 64, 128), BF16),
)
WORK = dict(
    wg_t=((128, 128), BF16),
    w1_t=((64, 64), BF16),
    w2_b=((8, 512), BF16),
    g_a=((128, 128), F32),
    g_b=((128, 128), F32),
    g_c=((128, 128), F32),
    q_t=((64, 128), F32),
    q_mul=((64, 60), F32),
    q_add=((64, 60), F32),
    k_row=((8, 128), F32),
    expanded=((64, 128), F32),
    logits=((4, 1024, 128), F32),
    q_f=((64, 640), F32),
    k_f=((128, 640), F32),
    q_p=((64, 512), BF16),
    k_p=((128, 512), BF16),
    v_p=((128, 512), BF16),
    coef=((64, 128), F32),
    pad=((128, 128), F32),
    pad_t=((128, 128), F32),
    own=((4, 640), BF16),
    q_nodes=((16, 4, 640), BF16),
    k_nodes=((32, 4, 640), BF16),
    att_s=((16, 4, 512), BF16),
    lse_s=((16, 4, 128), F32),
    att_r=((16, 4, 512), BF16),
    lse_r=((16, 4, 128), F32),
)


class Refs:
    pass


def own_block(w):
    w.own[:, 0:512] = layer_norm(w.nodes[...], w.ln_gain[...])
    w.pad[...] = jnp.zeros((128, 128), F32)
    rest = w.coords[...]
    for part in range(3):
        piece = rest.astype(BF16).astype(F32)
        w.pad[8 * part : 8 * part + 3, 0:4] = piece
        rest = rest - piece
    kinds = w.types[...] + w.gauss_mul.shape[0] // 2 * w.segments[...]
    w.pad[3:4, 0:4] = kinds.astype(F32)
    w.pad_t[...] = w.pad[...].T
    w.own[:, 512:640] = w.pad_t[0:4, :].astype(BF16)


def kernel(rows, cols, *refs):
    w = Refs()
    count = len(LOADED)
    sources, refs = refs[:count], refs[count:]
    w.attended, w.moved = refs[:2]
    refs = refs[2:]
    for name, ref in zip([*LOADED, *WORK], refs):
        setattr(w, name, ref)
    load_sem, kz_send, kz_recv, kx_send, kx_recv, qn_send, qn_recv = refs[-11:-4]
    at_send, at_recv, ls_send, ls_recv = refs[-4:]
    w.atoms = float(rows * cols * 4)
    row, col = lax.axis_index("row"), lax.axis_index("col")
    x, line = lax.rem(row, 4), lax.rem(row // 4, 2)
    level, core = col // 2, lax.rem(col, 2)
    home = row // 2
    own_key = home == col
    relay = core == x // 2
    half = lax.rem(x, 2)
    planes = rows // 4
    source_row = level * 4 + x

    def with_x(other):
        return row - x + other

    barrier = pltpu.get_barrier_semaphore()

    def greet(r, c):
        pl.semaphore_signal(barrier, inc=1, device_id=(r, c), device_id_type=MESH)

    def greet_row(n, carry):
        greet(row, lax.rem(col + n, cols))
        return carry

    @pl.when(relay)
    def _():
        def greet_source(n, carry):
            @pl.when(jnp.logical_not(jnp.logical_and(source_row == row, n == col)))
            def _():
                greet(source_row, n)

            return carry

        lax.fori_loop(0, cols, greet_source, 0)

    lax.fori_loop(1, cols, greet_row, 0)
    for side in range(2):
        other = 2 * core + side

        @pl.when(other != x)
        def _(other=other):
            greet(with_x(other), col)

    loads = []
    for n, (name, source) in enumerate(zip(LOADED, sources, strict=True)):
        loads.append(pltpu.make_async_copy(source, getattr(w, name), load_sem.at[n]))
        loads[-1].start()
    for load in loads[:5]:
        load.wait()
    own_block(w)

    pl.semaphore_wait(
        barrier, cols - 1 + planes - jnp.where(own_key, 1, 0) + jnp.where(relay, 3, 0)
    )

    def far_copy(n):
        plane = lax.rem(row // 4 + n, planes)
        return pltpu.make_async_remote_copy(
            src_ref=w.own,
            dst_ref=w.k_nodes.at[half * cols + col],
            send_sem=kz_send.at[n],
            recv_sem=kz_recv.at[col],
            device_id=(plane * 4 + x, home),
            device_id_type=MESH,
        )

    def far_copies(act):
        for n in [*range(planes // 2 + 1, 0, -2), *range(planes - 1, planes // 2 + 1, -2)]:
            act(far_copy(n))
        for n in range(planes // 2, 0, -2):
            act(far_copy(n))
        for n in range(planes - 2, planes // 2, -2):
            act(far_copy(n))

        @pl.when(jnp.logical_not(own_key))
        def _():
            act(far_copy(0))

    def relay_copy(pair, step):
        part = w.k_nodes.at[pl.ds(half * cols + 2 * pair, 2)]
        return pltpu.make_async_remote_copy(
            src_ref=part,
            dst_ref=part,
            send_sem=kx_send.at[pair * 3 + step - 1],
            recv_sem=kx_recv.at[half * (cols // 2) + pair],
            device_id=(with_x(lax.rem(x + step, 4)), col),
            device_id_type=MESH,
        )

    def row_copy(src, dst, send, recv, n):
        c = lax.rem(col + cols - n, cols)
        return pltpu.make_async_remote_copy(
            src_ref=src(c),
            dst_ref=dst.at[col],
            send_sem=send.at[n],
            recv_sem=recv.at[col],
            device_id=(row, c),
            device_id_type=MESH,
        )

    def row_copies(src, dst, send, recv, act):
        def one(n, carry):
            act(row_copy(src, dst, send, recv, n))
            return carry

        lax.fori_loop(1, cols, one, 0)

    def start(copy):
        copy.start()

    def sent(copy):
        copy.wait_send()

    def wait_row(src, dst, recv):
        def one(n, carry):
            c = lax.rem(col + n, cols)
            pltpu.make_async_copy(src(c), dst.at[c], recv.at[c]).wait()
            return carry

        lax.fori_loop(1, cols, one, 0)

    nod = lambda c: w.own
    far_copies(start)
    row_copies(nod, w.q_nodes, qn_send, qn_recv, start)
    w.q_nodes[col] = w.own[...]

    @pl.when(own_key)
    def _():
        w.k_nodes[half * cols + col] = w.own[...]

    for load in loads[5:-2]:
        load.wait()
    prepare(w)

    @pl.when(relay)
    def _():
        def forward(n, carry):
            m = jnp.where(line == lax.rem(level, 2), n, cols // 2 - 1 - n)
            shift = (m + 1) // 2 * (2 * lax.rem(m, 2) - 1)
            pair = lax.rem(level + shift + cols // 2, cols // 2)
            for side in range(2):
                c = 2 * pair + side

                @pl.when(jnp.logical_not(jnp.logical_and(own_key, c == col)))
                def _(c=c):
                    into = w.k_nodes.at[half * cols + c]
                    pltpu.make_async_copy(w.own, into, kz_recv.at[c]).wait()

            for step in range(1, 4):
                relay_copy(pair, step).start()
            return carry

        lax.fori_loop(0, cols // 2, forward, 0)

    wait_row(nod, w.q_nodes, qn_recv)
    for load in loads[-2:]:
        load.wait()
    query_side(w)
    for side in range(2):

        @pl.when(jnp.logical_not(jnp.logical_and(relay, half == side)))
        def _(side=side):
            def arrive(pair, carry):
                part = w.k_nodes.at[pl.ds(side * cols + 2 * pair, 2)]
                pltpu.make_async_copy(part, part, kx_recv.at[side * (cols // 2) + pair]).wait()
                return carry

            lax.fori_loop(0, cols // 2, arrive, 0)

    pair_distances(w)
    project(w)

    def out_copy(src, dst, send, recv, c):
        return pltpu.make_async_remote_copy(
            src_ref=src.at[c],
            dst_ref=dst.at[col],
            send_sem=send.at[c],
            recv_sem=recv.at[col],
            device_id=(row, c),
            device_id_type=MESH,
        )

    def out_copies(q, src, dst, send, recv):
        for s in range(4):
            c = 4 * q + s
            if q is not mine:
                out_copy(src, dst, send, recv, c).start()
                continue

            @pl.when(c != col)
            def _(c=c):
                out_copy(src, dst, send, recv, c).start()

    mine = level // 2
    far = mine // 2
    for n, q in enumerate((3 - 3 * far, 2 - far, mine + 1 - 2 * lax.rem(mine, 2), mine)):
        logits = w.logits.at[n]
        geometry(w, q, logits)
        stat = attention(w, q, logits)
        out_copies(q, w.att_s, w.att_r, at_send, at_recv)
        displacement(w, q, logits, stat)
        out_copies(q, w.lse_s, w.lse_r, ls_send, ls_recv)
    w.att_r[col] = w.att_s[col]
    w.lse_r[col] = w.lse_s[col]
    far_copies(sent)
    row_copies(nod, w.q_nodes, qn_send, qn_recv, sent)

    @pl.when(relay)
    def _():
        def drain(n, carry):
            for step in range(1, 4):
                relay_copy(n, step).wait_send()
            return carry

        lax.fori_loop(0, cols // 2, drain, 0)

    def finish(n, carry):
        c = lax.rem(col + n, cols)
        for src, dst, send, recv in (
            (w.att_s, w.att_r, at_send, at_recv),
            (w.lse_s, w.lse_r, ls_send, ls_recv),
        ):
            out_copy(src, dst, send, recv, c).wait_send()
            pltpu.make_async_copy(src.at[c], dst.at[c], recv.at[c]).wait()
        return carry

    lax.fori_loop(1, cols, finish, 0)
    w.attended[...] = combine_attended(w)
    w.moved[...] = combine_moved(w)


def hand_over(attended_from, moved_from, attended, moved):
    attended[...] = attended_from[...]
    moved[...] = moved_from[...]


def shards(
    nodes,
    coords,
    atom_types,
    segment_ids,
    pair_mask,
    pair_bias,
    ln_gain,
    w_qkv,
    gauss_mul,
    gauss_add,
    gauss_mean,
    gauss_width,
    w_gauss,
    w_heads,
    w_coord1,
    w_coord2,
    *,
    rows,
    cols,
):
    vmem = pl.BlockSpec(memory_space=pltpu.VMEM)
    hbm = pl.BlockSpec(memory_space=pl.ANY)
    dma = lambda n: pltpu.SemaphoreType.DMA((n,))
    outs = (
        jax.ShapeDtypeStruct(nodes.shape, BF16),
        jax.ShapeDtypeStruct(coords.shape, F32),
    )
    results = pl.pallas_call(
        functools.partial(kernel, rows, cols),
        out_shape=outs,
        in_specs=[hbm] * len(LOADED),
        out_specs=(vmem, vmem),
        scratch_shapes=[pltpu.VMEM(*spec) for spec in [*LOADED.values(), *WORK.values()]]
        + [dma(len(LOADED)), dma(rows // 4), dma(cols), dma(3 * cols // 2), dma(cols)]
        + [dma(cols)] * 6,
        compiler_params=pltpu.CompilerParams(collective_id=0, has_side_effects=True),
        name="refine",
    )(
        nodes,
        coords,
        atom_types[None],
        segment_ids[None],
        ln_gain[None],
        gauss_mean[None],
        gauss_width[None],
        w_gauss,
        w_coord1,
        w_coord2[None],
        gauss_mul,
        gauss_add,
        w_heads.T,
        pair_mask,
        w_qkv,
        pair_bias,
    )
    return pl.pallas_call(
        hand_over,
        out_shape=outs,
        in_specs=[vmem, vmem],
        out_specs=(vmem, vmem),
        name="hand_over",
    )(*results)


def solution(mesh):
    in_specs = (
        P(("row", "col"), None),
        P(None, ("row", "col")),
        P(("row", "col")),
        P(("row", "col")),
        P("row", "col"),
        P(None, "row", "col"),
    ) + (P(),) * 10
    out_specs = (P(("row", "col"), None), P(None, ("row", "col")))
    body = functools.partial(shards, rows=mesh.shape["row"], cols=mesh.shape["col"])
    return jax.shard_map(body, mesh=mesh, in_specs=in_specs, out_specs=out_specs, check_vma=False)
```
